32 devices in a mesh: row: 8 (over z, core), col: 4 (over y, x).
Axes of the slice: x: 2, y: 2, z: 4, core: 2. Of those that a mesh axis runs over, the one named last changes fastest.
Arguments:
- pair_elems: bfloat16 [320, 12288], P('row', 'col'), may hold values from -0.59765625 to 0.59765625
- counts: int32 [8], replicated, may hold values from 1 to 40, 200 in all
- val_band: int32 [320], replicated, may hold values from 0 to 127
- cond_band: int32 [320], replicated, may hold values from 0 to 511
- val_energy: float32 [128], replicated, may hold values from -12 to -0.5
- cond_energy: float32 [512], replicated, may hold values from 0.5 to 12
- frequency: float32 [3], replicated, may hold values from 0.3 to 6
Outputs:
- chi: float32 [3, 12288, 12288], P(None, 'row', 'col')
The draws below stay inside these ranges and needn't reach their ends.
Inputs may be any that keep to these rules, and one draw needn't show every extreme that they name: counts sum to 200, and the largest is 40.
All inputs are finite; a program needn't handle non-finite values.
Results may differ from the reference program's by a relative error of at most 0.0028.
Values may be sent and summed in bfloat16 or wider, within the bound.
A program may use at most 128 MiB of HBM per device.

```python
import math
import jax
import jax.numpy as jnp
import numpy as np
from jax import lax

NPW = 12288
NVAL = 128
NCOND = 512
NFREQ = 3
CAP = 40
SLOTS = 320
TOTAL = 200
N_ROW = 8


def touch_ends(result, rng, smallest, largest):
    place = [jax.random.randint(jax.random.fold_in(rng, axis), (), 0, length) for axis, length in enumerate(result.shape)]
    widest = result.shape.index(max(result.shape))
    neighbour = place[:widest] + [(place[widest] + 1) % result.shape[widest]] + place[widest + 1:]
    return result.at[tuple(place)].set(smallest).at[tuple(neighbour)].set(largest)


def levels(rng, extent, cuts, least, top_value):
    loudness = 1.0
    for dim, shards_of in cuts:
        heights = jax.random.uniform(jax.random.fold_in(jax.random.fold_in(rng, 6), dim), (shards_of,), jnp.float32, least / len(cuts), top_value / len(cuts))
        loudness = loudness * jnp.repeat(jnp.exp(heights), extent[dim] // shards_of).reshape((-1,) + (1,) * (len(extent) - 1 - dim))
    return loudness


def profile(count, total, bound, slope):
    portions = [(1 << 20) // math.isqrt(rank ** slope) + 1 for rank in range(2, count + 1)]
    rest, holding = total - bound - (count - 1), [1] * (count - 1)
    while rest > 0:
        movable = [i for i in range(count - 1) if holding[i] < bound]
        mass, left = sum([portions[i] for i in movable]), rest
        for i in movable:
            more = min(bound - holding[i], max(1, left * portions[i] // mass), rest)
            holding[i] = holding[i] + more
            rest = rest - more
    return np.array([bound] + holding)


def ragged(rng, amount, total, reach, slope):
    if amount == 2:
        one = jax.random.randint(rng, (), max(1, total - reach), min(reach, total - 1) + 1)
        return jnp.stack([one, total - one])
    lengths = jnp.asarray(profile(amount, total, reach, slope), jnp.int32)
    pairs = (amount - 1) // 2
    donor, sink = lengths[1:1 + 2 * pairs:2], lengths[2:2 + 2 * pairs:2]
    margin = jnp.minimum(donor - 1, reach - sink)
    moved = jax.random.randint(jax.random.fold_in(rng, 1), (pairs,), 0, 1 << 20) % (margin + 1)
    lengths = lengths.at[1:1 + 2 * pairs:2].set(donor - moved).at[2:2 + 2 * pairs:2].set(sink + moved)
    return lengths[jax.random.permutation(jax.random.fold_in(rng, 2), amount)]


def normal_values(key, extent, spread, limit, shards=(), kind=jnp.bfloat16):
    entries = jax.random.normal(key, extent, jnp.float32) * spread
    if len(shards) > 0:
        entries = levels(key, extent, shards, -0.22, 0.18) * entries
    return jnp.clip(entries, min=-limit, max=limit).astype(kind)


def setup_inputs(seed: int = 0) -> dict:
    seeds = jax.random.split(jax.random.key(seed), 8)
    pair_elems = normal_values(seeds[0], (SLOTS, NPW), 0.1, 0.59765625, ((0, 8), (1, 4)))
    counts = ragged(seeds[1], N_ROW, TOTAL, CAP, 2).astype(jnp.int32)
    val_band = touch_ends(jax.random.randint(seeds[2], (SLOTS,), 0, NVAL), jax.random.fold_in(seeds[2], 1), 0, NVAL - 1).astype(jnp.int32)
    cond_band = touch_ends(jax.random.randint(seeds[3], (SLOTS,), 0, NCOND), jax.random.fold_in(seeds[3], 1), 0, NCOND - 1).astype(jnp.int32)
    val_energy = jnp.clip(jax.random.uniform(seeds[4], (NVAL,), jnp.float32, -12.0, -0.5), -12.0, -0.5)
    cond_energy = jnp.clip(jax.random.uniform(seeds[5], (NCOND,), jnp.float32, 0.5, 12.0), 0.5, 12.0)
    frequency = jnp.clip(jnp.exp(jax.random.uniform(seeds[6], (NFREQ,), jnp.float32, math.log(0.3), math.log(6.0))), 0.3, 6.0)
    return dict(pair_elems=pair_elems, counts=counts, val_band=val_band, cond_band=cond_band, val_energy=val_energy, cond_energy=cond_energy, frequency=frequency)


def reference(pair_elems, counts, val_band, cond_band, val_energy, cond_energy, frequency):
    live_mask = (jnp.arange(CAP, dtype=jnp.int32)[None, :] < counts[:, None]).astype(jnp.float32).reshape(-1)
    energy_gap = jnp.take(cond_energy, cond_band) - jnp.take(val_energy, val_band)
    weights = -4.0 * live_mask[None, :] * energy_gap[None, :] / (energy_gap[None, :] ** 2 + frequency[:, None] ** 2)
    elements = pair_elems.astype(jnp.float32)

    def one_frequency(weight_row):
        scaled = (elements * weight_row[:, None]).astype(jnp.bfloat16)
        return lax.dot_general(scaled, pair_elems, (((0,), (0,)), ((), ())), preferred_element_type=jnp.float32)

    return lax.map(one_frequency, weights)
```

```python
import functools

import jax
import jax.numpy as jnp
from jax import lax
from jax.experimental import pallas as pl
from jax.experimental.pallas import tpu as pltpu
from jax.sharding import PartitionSpec as P

MESH = pl.DeviceIdType.MESH
LAG = 2


def ring_place(c, count):
    if count == 4:
        return c + (c // 2) * (1 - 2 * (c % 2))
    return c


def gather_kernel(rows, cols, halves, x_ref, cols_ref, seg_ref, own_sem, line_send, line_recv, mate_send, mate_recv,
                  enter_send, relay_send, ring_recv):
    r, c = lax.axis_index("row"), lax.axis_index("col")
    chips = rows // 2
    q, k = r // 2, r % 2
    width = x_ref.shape[1]
    ratio = rows // cols
    seg_width = width // ratio
    chunk = seg_width // halves
    chunks = ratio * halves
    lane = chunk // 2
    place = ring_place(c, cols)
    source = r // ratio
    ring_next = [ring_place((place + 1) % cols, cols), ring_place((place + cols - 1) % cols, cols)]
    up_ok, down_ok = q + 1 < chips, q >= 1

    own = pltpu.make_async_copy(x_ref, cols_ref.at[r], own_sem)
    own.start()
    barrier = pltpu.get_barrier_semaphore()

    def greet(row, col):
        pl.semaphore_signal(barrier, inc=1, device_id=(row, col), device_id_type=MESH)

    mate = 2 * q + 1 - k
    greet(mate, c)
    for nxt in ring_next:
        greet(2 * q, nxt)
        greet(2 * q + 1, nxt)

    @pl.when(up_ok)
    def _():
        greet(r + 2, c)

    @pl.when(down_ok)
    def _():
        greet(r - 2, c)

    pl.semaphore_wait(barrier, 5 + up_ok.astype(jnp.int32) + down_ok.astype(jnp.int32))
    own.wait()

    def remote(src, dst, send, recv, row, col):
        return pltpu.make_async_remote_copy(
            src_ref=src, dst_ref=dst, send_sem=send, recv_sem=recv, device_id=(row, col), device_id_type=MESH
        )

    def span(start, size):
        return pl.ds(pl.multiple_of(start, 128), size)

    def block_of(stream, d, core):
        return 2 * (q - d if stream == 0 else q + d) + core

    def has(stream, d):
        return q >= d if stream == 0 else q + d < chips

    def line_copy(stream, d, j, b):
        ref = cols_ref.at[b, :, span(j * chunk, chunk)]
        row = r + 2 if stream == 0 else r - 2
        return remote(ref, ref, line_send.at[stream, d, j], line_recv.at[stream, d, j], row, c)

    def line_arrival(stream, d, j, b):
        ref = cols_ref.at[b, :, span(j * chunk, chunk)]
        return remote(ref, ref, line_send.at[stream, d, j], line_recv.at[stream, d - 1, j], mate, c)

    def mate_copy(b, j):
        ref = cols_ref.at[b, :, span(j * chunk, chunk)]
        return remote(ref, ref, mate_send.at[b, j], mate_recv.at[b, j], mate, c)

    def enter_copy(b, j, way):
        g = c * ratio + j // halves
        src = cols_ref.at[b, :, span(j * chunk + way * lane, lane)]
        dst = seg_ref.at[b, :, span((j % halves) * chunk + way * lane, lane)]
        return remote(src, dst, enter_send.at[b, j, way], ring_recv.at[b, j % halves, way], g, ring_next[way])

    def relay_copy(b, j, way):
        ref = seg_ref.at[b, :, span((j % halves) * chunk + way * lane, lane)]
        return remote(ref, ref, relay_send.at[b, j % halves, way], ring_recv.at[b, j % halves, way], r, ring_next[way])

    def feeds(j):
        return (c * ratio + j // halves) // 2 == q

    def relays(j):
        return (source != c) & (j // halves == r % ratio)

    def onward(stream):
        return up_ok if stream == 0 else down_ok

    def line_part(step):
        j, d = step // chips, step % chips
        for stream in (0, 1):
            here = has(stream, d) if stream == 0 else has(stream, d) & (d > 0)
            b = block_of(stream, d, k)

            @pl.when(has(stream, d))
            def _():
                @pl.when(d > 0)
                def _():
                    line_arrival(stream, d, j, b).wait_recv()

                @pl.when(onward(stream))
                def _():
                    line_copy(stream, d, j, b).start()

            @pl.when(here)
            def _():
                mate_copy(b, j).start()

                @pl.when(feeds(j))
                def _():
                    for way in (0, 1):
                        enter_copy(b, j, way).start()

    def ring_part(step):
        j, d = step // chips, step % chips

        @pl.when(relays(j))
        def _():
            for stream in (0, 1):
                here = has(stream, d) if stream == 0 else has(stream, d) & (d > 0)

                @pl.when(here)
                def _():
                    for core in (0, 1):
                        b = block_of(stream, d, core)
                        for way in (0, 1):
                            relay_copy(b, j, way).wait_recv()

                            @pl.when(ring_next[way] != source)
                            def _():
                                relay_copy(b, j, way).start()

    steps = chunks * chips

    def body(step, carry):
        @pl.when(step < steps)
        def _():
            line_part(step)

        @pl.when(step >= LAG)
        def _():
            ring_part(step - LAG)

        return carry

    lax.fori_loop(0, steps + LAG, body, 0)

    def finish(step, carry):
        j, d = step // chips, step % chips
        for stream in (0, 1):
            here = has(stream, d) if stream == 0 else has(stream, d) & (d > 0)
            b = block_of(stream, d, k)
            theirs = block_of(stream, d, 1 - k)

            @pl.when(has(stream, d) & onward(stream))
            def _():
                line_copy(stream, d, j, b).wait_send()

            @pl.when(here)
            def _():
                mate_copy(b, j).wait_send()
                mate_copy(theirs, j).wait_recv()

                @pl.when(feeds(j))
                def _():
                    for way in (0, 1):
                        enter_copy(b, j, way).wait_send()

                @pl.when(relays(j))
                def _():
                    for core in (0, 1):
                        e = block_of(stream, d, core)
                        for way in (0, 1):
                            @pl.when(ring_next[way] != source)
                            def _():
                                relay_copy(e, j, way).wait_send()

        return carry

    lax.fori_loop(0, steps, finish, 0)

    @pl.when(source == c)
    def _():
        here = pltpu.make_async_copy(cols_ref.at[:, :, span((r % ratio) * seg_width, seg_width)], seg_ref, own_sem)
        here.start()
        here.wait()


def gather(x, rows, cols):
    capacity, width = x.shape
    ratio = rows // cols
    seg_width = width // ratio
    halves = 2 if seg_width % 512 == 0 else 1
    chunks, chips = ratio * halves, rows // 2
    dma = pltpu.SemaphoreType.DMA
    return pl.pallas_call(
        functools.partial(gather_kernel, rows, cols, halves),
        out_shape=(
            jax.ShapeDtypeStruct((rows, capacity, width), x.dtype),
            jax.ShapeDtypeStruct((rows, capacity, seg_width), x.dtype),
        ),
        in_specs=[pl.BlockSpec(memory_space=pl.ANY)],
        out_specs=(pl.BlockSpec(memory_space=pltpu.VMEM), pl.BlockSpec(memory_space=pltpu.VMEM)),
        scratch_shapes=[
            dma,
            dma((2, chips, chunks)),
            dma((2, chips, chunks)),
            dma((rows, chunks)),
            dma((rows, chunks)),
            dma((rows, chunks, 2)),
            dma((rows, halves, 2)),
            dma((rows, halves, 2)),
        ],
        compiler_params=pltpu.CompilerParams(collective_id=0, has_side_effects=True),
    )(x)


def product_kernel(weights_ref, seg_ref, cols_ref, out_ref):
    which = pl.program_id(1)
    slots, width = weights_ref.shape[1], cols_ref.shape[2]
    weight = weights_ref[which]
    seg = seg_ref[...].reshape(slots, seg_ref.shape[2]).astype(jnp.float32)
    scaled = (seg * weight).astype(jnp.bfloat16)
    columns = cols_ref[...].reshape(slots, width)
    out_ref[0] = lax.dot_general(
        scaled, columns, (((0,), (0,)), ((), ())), preferred_element_type=jnp.float32
    )


def product(weights, seg, columns):
    freqs = weights.shape[0]
    rows, capacity, seg_width = seg.shape
    width = columns.shape[2]
    slots = rows * capacity
    tile = 256
    return pl.pallas_call(
        product_kernel,
        out_shape=jax.ShapeDtypeStruct((freqs, seg_width, width), jnp.float32),
        grid=(seg_width // tile, freqs),
        in_specs=[
            pl.BlockSpec((freqs, slots, 1), lambda m, f: (0, 0, 0), pipeline_mode=pl.Buffered(1)),
            pl.BlockSpec((rows, capacity, tile), lambda m, f: (0, 0, m)),
            pl.BlockSpec((rows, capacity, width), lambda m, f: (0, 0, 0), pipeline_mode=pl.Buffered(1)),
        ],
        out_specs=pl.BlockSpec((1, tile, width), lambda m, f: (f, m, 0)),
        compiler_params=pltpu.CompilerParams(vmem_limit_bytes=48 * 1024 * 1024),
    )(weights[:, :, None], seg, columns)


def lookup_energy(band, table):
    levels = jnp.arange(table.shape[0], dtype=jnp.int32)
    return jnp.sum(jnp.where(band[:, None] == levels[None, :], table[None, :], 0.0), axis=1)


def per_device(pair_elems, counts, val_band, cond_band, val_energy, cond_energy, frequency):
    capacity = pair_elems.shape[0]
    rows, cols = lax.axis_size("row"), lax.axis_size("col")
    position = jnp.arange(rows * capacity, dtype=jnp.int32)
    limits = jnp.repeat(counts, capacity)
    live_mask = (position % capacity < limits).astype(jnp.float32)
    energy_gap = lookup_energy(cond_band, cond_energy) - lookup_energy(val_band, val_energy)
    weights = (
        -4.0
        * live_mask[None, :]
        * energy_gap[None, :]
        / (energy_gap[None, :] ** 2 + frequency[:, None] ** 2)
    )
    columns, seg = gather(pair_elems, rows, cols)
    return product(weights, seg, columns)


def solution(mesh):
    in_specs = (P("row", "col"), P(), P(), P(), P(), P(), P())
    out_specs = P(None, "row", "col")
    return jax.shard_map(
        per_device, mesh=mesh, in_specs=in_specs, out_specs=out_specs, check_vma=False
    )
```

```python
import functools

import jax
import jax.numpy as jnp
from jax import lax
from jax.experimental import pallas as pl
from jax.experimental.pallas import tpu as pltpu
from jax.sharding import PartitionSpec as P

MESH = pl.DeviceIdType.MESH
LAG = 3


def ring_place(c, count):
    if count == 4:
        return c + (c // 2) * (1 - 2 * (c % 2))
    return c


def gather_kernel(rows, cols, halves, x_ref, cols_ref, seg_ref, own_sem, line_send, line_recv, mate_send, mate_recv,
                  enter_send, relay_send, ring_recv):
    r, c = lax.axis_index("row"), lax.axis_index("col")
    chips = rows // 2
    q, k = r // 2, r % 2
    pieces, lane = cols_ref.shape[1], cols_ref.shape[3]
    ratio = rows // cols
    chunks = ratio * halves
    place = ring_place(c, cols)
    source = r // ratio
    ring_next = [ring_place((place + 1) % cols, cols), ring_place((place + cols - 1) % cols, cols)]
    ahead = (place - ring_place(source, cols) + cols) % cols
    hops = [ahead, cols - ahead]
    up_ok, down_ok = q + 1 < chips, q >= 1

    own = [
        pltpu.make_async_copy(x_ref.at[:, pl.ds(p * lane, lane)], cols_ref.at[r, p], own_sem.at[p])
        for p in range(pieces)
    ]
    for copy in own:
        copy.start()
    barrier = pltpu.get_barrier_semaphore()

    def greet(row, col):
        pl.semaphore_signal(barrier, inc=1, device_id=(row, col), device_id_type=MESH)

    mate = 2 * q + 1 - k
    greet(mate, c)
    for nxt in ring_next:
        greet(2 * q, nxt)
        greet(2 * q + 1, nxt)

    @pl.when(up_ok)
    def _():
        greet(r + 2, c)

    @pl.when(down_ok)
    def _():
        greet(r - 2, c)

    pl.semaphore_wait(barrier, 5 + up_ok.astype(jnp.int32) + down_ok.astype(jnp.int32))
    for copy in own:
        copy.wait()

    def remote(src, dst, send, recv, row, col):
        return pltpu.make_async_remote_copy(
            src_ref=src, dst_ref=dst, send_sem=send, recv_sem=recv, device_id=(row, col), device_id_type=MESH
        )

    def block_of(stream, d, core):
        return 2 * (q - d if stream == 0 else q + d) + core

    def has(stream, d):
        return q >= d if stream == 0 else q + d < chips

    def line_copy(stream, d, j, b):
        ref = cols_ref.at[b, pl.ds(2 * j, 2)]
        row = r + 2 if stream == 0 else r - 2
        return remote(ref, ref, line_send.at[stream, d, j], line_recv.at[stream, d, j], row, c)

    def line_arrival(stream, d, j, b):
        ref = cols_ref.at[b, pl.ds(2 * j, 2)]
        return remote(ref, ref, line_send.at[stream, d, j], line_recv.at[stream, d - 1, j], mate, c)

    def mate_copy(b, j):
        ref = cols_ref.at[b, pl.ds(2 * j, 2)]
        return remote(ref, ref, mate_send.at[b, j], mate_recv.at[b, j], mate, c)

    def enter_copy(b, j, way):
        g = c * ratio + j // halves
        src = cols_ref.at[b, 2 * j + way]
        dst = seg_ref.at[b, 2 * (j % halves) + way]
        return remote(src, dst, enter_send.at[b, j, way], ring_recv.at[b, j % halves, way], g, ring_next[way])

    def relay_copy(b, j, way):
        ref = seg_ref.at[b, 2 * (j % halves) + way]
        return remote(ref, ref, relay_send.at[b, j % halves, way], ring_recv.at[b, j % halves, way], r, ring_next[way])

    def feeds(j):
        return (c * ratio + j // halves) // 2 == q

    def relays(j):
        return (source != c) & (j // halves == r % ratio)

    def onward(stream):
        return up_ok if stream == 0 else down_ok

    def line_part(step):
        d, j = step // chunks, step % chunks
        for stream in (0, 1):
            here = has(stream, d) if stream == 0 else has(stream, d) & (d > 0)
            b = block_of(stream, d, k)

            @pl.when(has(stream, d))
            def _():
                @pl.when(d > 0)
                def _():
                    line_arrival(stream, d, j, b).wait_recv()

                @pl.when(onward(stream))
                def _():
                    line_copy(stream, d, j, b).start()

            @pl.when(here)
            def _():
                mate_copy(b, j).start()

                @pl.when(feeds(j))
                def _():
                    for way in (0, 1):
                        enter_copy(b, j, way).start()

    def ring_part(step, way):
        d, j = step // chunks, step % chunks

        @pl.when(relays(j))
        def _():
            for stream in (0, 1):
                here = has(stream, d) if stream == 0 else has(stream, d) & (d > 0)

                @pl.when(here)
                def _():
                    for core in (0, 1):
                        b = block_of(stream, d, core)
                        relay_copy(b, j, way).wait_recv()

                        @pl.when(ring_next[way] != source)
                        def _():
                            relay_copy(b, j, way).start()

    steps = chunks * chips

    def body(step, carry):
        @pl.when(step < steps)
        def _():
            line_part(step)

        for way in (0, 1):
            late = step - LAG * hops[way]

            @pl.when((late >= 0) & (late < steps))
            def _():
                ring_part(late, way)

        return carry

    lax.fori_loop(0, steps + LAG * (cols - 1), body, 0)

    def finish(step, carry):
        d, j = step // chunks, step % chunks
        for stream in (0, 1):
            here = has(stream, d) if stream == 0 else has(stream, d) & (d > 0)
            b = block_of(stream, d, k)
            theirs = block_of(stream, d, 1 - k)

            @pl.when(has(stream, d) & onward(stream))
            def _():
                line_copy(stream, d, j, b).wait_send()

            @pl.when(here)
            def _():
                mate_copy(b, j).wait_send()
                mate_copy(theirs, j).wait_recv()

                @pl.when(feeds(j))
                def _():
                    for way in (0, 1):
                        enter_copy(b, j, way).wait_send()

                @pl.when(relays(j))
                def _():
                    for core in (0, 1):
                        e = block_of(stream, d, core)
                        for way in (0, 1):
                            @pl.when(ring_next[way] != source)
                            def _():
                                relay_copy(e, j, way).wait_send()

        return carry

    lax.fori_loop(0, steps, finish, 0)

    @pl.when(source == c)
    def _():
        here = pltpu.make_async_copy(cols_ref.at[:, pl.ds((r % ratio) * 2 * halves, 2 * halves)], seg_ref, own_sem.at[0])
        here.start()
        here.wait()


def gather(x, rows, cols):
    capacity, width = x.shape
    ratio = rows // cols
    seg_width = width // ratio
    halves = 2 if seg_width % 512 == 0 else 1
    chunks, chips = ratio * halves, rows // 2
    dma = pltpu.SemaphoreType.DMA
    return pl.pallas_call(
        functools.partial(gather_kernel, rows, cols, halves),
        out_shape=(
            jax.ShapeDtypeStruct((rows, 2 * chunks, capacity, seg_width // halves // 2), x.dtype),
            jax.ShapeDtypeStruct((rows, 2 * halves, capacity, seg_width // halves // 2), x.dtype),
        ),
        in_specs=[pl.BlockSpec(memory_space=pl.ANY)],
        out_specs=(pl.BlockSpec(memory_space=pltpu.VMEM), pl.BlockSpec(memory_space=pltpu.VMEM)),
        scratch_shapes=[
            dma((2 * chunks,)),
            dma((2, chips, chunks)),
            dma((2, chips, chunks)),
            dma((rows, chunks)),
            dma((rows, chunks)),
            dma((rows, chunks, 2)),
            dma((rows, halves, 2)),
            dma((rows, halves, 2)),
        ],
        compiler_params=pltpu.CompilerParams(collective_id=0, has_side_effects=True),
    )(x)


def exact_dot(a, b):
    return lax.dot_general(
        a, b, (((1,), (0,)), ((), ())), precision=lax.Precision.HIGHEST, preferred_element_type=jnp.float32
    )


def pick(band_ref, table_ref):
    levels, slots = table_ref.shape[1], band_ref.shape[1]
    hit = lax.broadcasted_iota(jnp.int32, (levels, slots), 0) == band_ref[...]
    return exact_dot(jnp.broadcast_to(table_ref[...], (8, levels)), hit.astype(jnp.float32))


def slot_target(counts_ref, shape, axis, capacity):
    slot = lax.broadcasted_iota(jnp.int32, shape, axis)
    target = jnp.full(shape, -1, jnp.int32)
    before = 0
    for block in range(counts_ref.shape[0]):
        inside = slot - block * capacity
        live = (inside >= 0) & (inside < counts_ref[block])
        target = jnp.where(live, inside + before, target)
        before = before + counts_ref[block]
    return target


def product_kernel(counts_ref, freq_ref, val_band, cond_band, val_energy, cond_energy, seg_ref, cols_ref, out_ref,
                   packed, turned, weights):
    which = pl.program_id(1)
    tile, (depth, width) = out_ref.shape[1], packed.shape
    rows, pieces, capacity, lane = cols_ref.shape
    slots = rows * capacity

    @pl.when((pl.program_id(0) == 0) & (which == 0))
    def _():
        place = slot_target(counts_ref, (1, slots), 1, capacity)
        choose = (lax.broadcasted_iota(jnp.int32, (depth, slots), 0) == place).astype(jnp.float32)
        gap = pick(cond_band, cond_energy) - pick(val_band, val_energy)
        gap = lax.dot_general(
            gap, choose, (((1,), (1,)), ((), ())), precision=lax.Precision.HIGHEST, preferred_element_type=jnp.float32
        )
        for f in range(weights.shape[0]):
            weights[f] = -4.0 * gap / (gap * gap + freq_ref[f] * freq_ref[f])
        choose = choose.astype(jnp.bfloat16)
        for p in range(pieces):
            piece = cols_ref[:, p].reshape(slots, lane)
            packed[:, p * lane : (p + 1) * lane] = jnp.dot(
                choose, piece, preferred_element_type=jnp.float32
            ).astype(jnp.bfloat16)
        for p in range(seg_ref.shape[1]):
            piece = seg_ref[:, p].reshape(slots, lane)
            turned[p * lane : (p + 1) * lane, :] = lax.dot_general(
                piece, choose, (((0,), (1,)), ((), ())), preferred_element_type=jnp.float32
            ).astype(jnp.bfloat16)

    start = pl.multiple_of(pl.program_id(0) * tile, tile)
    scaled = (turned[pl.ds(start, tile), :].astype(jnp.float32) * weights[which][:1]).astype(jnp.bfloat16)
    out_ref[0] = jnp.dot(scaled, packed[...], preferred_element_type=jnp.float32)


def product(counts, frequency, val_band, cond_band, val_energy, cond_energy, seg, columns):
    freqs = frequency.shape[0]
    rows, pieces, capacity, lane = columns.shape
    width, seg_width = pieces * lane, seg.shape[1] * lane
    slots = rows * capacity
    live = slots * 5 // 8
    depth = pl.cdiv(live, 256) * 256
    tile = 256
    smem, vmem = pl.BlockSpec(memory_space=pltpu.SMEM), pl.BlockSpec(memory_space=pltpu.VMEM)
    return pl.pallas_call(
        product_kernel,
        out_shape=jax.ShapeDtypeStruct((freqs, seg_width, width), jnp.float32),
        grid=(seg_width // tile, freqs),
        in_specs=[smem, smem, vmem, vmem, vmem, vmem, vmem, vmem],
        out_specs=pl.BlockSpec((1, tile, width), lambda m, f: (f, m, 0)),
        scratch_shapes=[
            pltpu.VMEM((depth, width), jnp.bfloat16),
            pltpu.VMEM((seg_width, depth), jnp.bfloat16),
            pltpu.VMEM((freqs, 8, depth), jnp.float32),
        ],
        compiler_params=pltpu.CompilerParams(vmem_limit_bytes=48 * 1024 * 1024),
    )(counts, frequency, val_band[None], cond_band[None], val_energy[None], cond_energy[None], seg, columns)


def per_device(pair_elems, counts, val_band, cond_band, val_energy, cond_energy, frequency):
    rows, cols = lax.axis_size("row"), lax.axis_size("col")
    columns, seg = gather(pair_elems, rows, cols)
    return product(counts, frequency, val_band, cond_band, val_energy, cond_energy, seg, columns)


def solution(mesh):
    in_specs = (P("row", "col"), P(), P(), P(), P(), P(), P())
    out_specs = P(None, "row", "col")
    return jax.shard_map(
        per_device, mesh=mesh, in_specs=in_specs, out_specs=out_specs, check_vma=False
    )
```

```python
import functools
import math

import jax
import jax.numpy as jnp
from jax import lax
from jax.experimental import pallas as pl
from jax.experimental.pallas import tpu as pltpu
from jax.sharding import PartitionSpec as P

MESH = pl.DeviceIdType.MESH
LAG = 3
TILE = 1024


def ring_place(c, count):
    if count == 4:
        return c + (c // 2) * (1 - 2 * (c % 2))
    return c


def gather_kernel(rows, cols, halves, x_ref, counts_hbm, freq_hbm, val_band_hbm, cond_band_hbm, val_energy_hbm,
                  cond_energy_hbm, cols_ref, seg_ref, choose_ref, weights_ref, counts_ref, freq_ref, val_band, cond_band,
                  val_energy, cond_energy, small_sem, own_sem, line_send, line_recv, mate_send, mate_recv, enter_send,
                  relay_send, ring_recv):
    r, c = lax.axis_index("row"), lax.axis_index("col")
    chips = rows // 2
    q, k = r // 2, r % 2
    pieces, lane = cols_ref.shape[1], cols_ref.shape[3]
    ratio = rows // cols
    chunks = ratio * halves
    place = ring_place(c, cols)
    source = r // ratio
    ring_next = [ring_place((place + 1) % cols, cols), ring_place((place + cols - 1) % cols, cols)]
    ahead = (place - ring_place(source, cols) + cols) % cols
    hops = [ahead, cols - ahead]
    up_ok, down_ok = q + 1 < chips, q >= 1

    own = [
        pltpu.make_async_copy(x_ref.at[:, pl.ds(p * lane, lane)], cols_ref.at[r, p], own_sem.at[p])
        for p in range(pieces)
    ]
    small = [
        pltpu.make_async_copy(src, dst, small_sem.at[i])
        for i, (src, dst) in enumerate((
            (counts_hbm, counts_ref), (freq_hbm, freq_ref), (val_band_hbm, val_band), (cond_band_hbm, cond_band),
            (val_energy_hbm, val_energy), (cond_energy_hbm, cond_energy),
        ))
    ]
    for copy in own + small:
        copy.start()
    barrier = pltpu.get_barrier_semaphore()

    def greet(row, col):
        pl.semaphore_signal(barrier, inc=1, device_id=(row, col), device_id_type=MESH)

    mate = 2 * q + 1 - k
    greet(mate, c)
    for nxt in ring_next:
        greet(2 * q, nxt)
        greet(2 * q + 1, nxt)

    @pl.when(up_ok)
    def _():
        greet(r + 2, c)

    @pl.when(down_ok)
    def _():
        greet(r - 2, c)

    pl.semaphore_wait(barrier, 5 + up_ok.astype(jnp.int32) + down_ok.astype(jnp.int32))
    for copy in own:
        copy.wait()

    def remote(src, dst, send, recv, row, col):
        return pltpu.make_async_remote_copy(
            src_ref=src, dst_ref=dst, send_sem=send, recv_sem=recv, device_id=(row, col), device_id_type=MESH
        )

    def block_of(stream, d, core):
        return 2 * (q - d if stream == 0 else q + d) + core

    def has(stream, d):
        return q >= d if stream == 0 else q + d < chips

    def line_copy(stream, d, j, b):
        ref = cols_ref.at[b, pl.ds(2 * j, 2)]
        row = r + 2 if stream == 0 else r - 2
        return remote(ref, ref, line_send.at[stream, d, j], line_recv.at[stream, d, j], row, c)

    def line_arrival(stream, d, j, b):
        ref = cols_ref.at[b, pl.ds(2 * j, 2)]
        return remote(ref, ref, line_send.at[stream, d, j], line_recv.at[stream, d - 1, j], mate, c)

    def mate_copy(b, j):
        ref = cols_ref.at[b, pl.ds(2 * j, 2)]
        return remote(ref, ref, mate_send.at[b, j], mate_recv.at[b, j], mate, c)

    def enter_copy(b, j, way):
        g = c * ratio + j // halves
        src = cols_ref.at[b, 2 * j + way]
        dst = seg_ref.at[b, 2 * (j % halves) + way]
        return remote(src, dst, enter_send.at[b, j, way], ring_recv.at[b, j % halves, way], g, ring_next[way])

    def relay_copy(b, j, way):
        ref = seg_ref.at[b, 2 * (j % halves) + way]
        return remote(ref, ref, relay_send.at[b, j % halves, way], ring_recv.at[b, j % halves, way], r, ring_next[way])

    def feeds(j):
        return (c * ratio + j // halves) // 2 == q

    def relays(j):
        return (source != c) & (j // halves == r % ratio)

    def onward(stream):
        return up_ok if stream == 0 else down_ok

    def line_part(step):
        d, j = step // chunks, step % chunks
        for stream in (0, 1):
            here = has(stream, d) if stream == 0 else has(stream, d) & (d > 0)
            b = block_of(stream, d, k)

            @pl.when(has(stream, d))
            def _():
                @pl.when(d > 0)
                def _():
                    line_arrival(stream, d, j, b).wait_recv()

                @pl.when(onward(stream))
                def _():
                    line_copy(stream, d, j, b).start()

            @pl.when(here)
            def _():
                mate_copy(b, j).start()

                @pl.when(feeds(j))
                def _():
                    for way in (0, 1):
                        enter_copy(b, j, way).start()

    def ring_part(step, way):
        d, j = step // chunks, step % chunks

        @pl.when(relays(j))
        def _():
            for stream in (0, 1):
                here = has(stream, d) if stream == 0 else has(stream, d) & (d > 0)

                @pl.when(here)
                def _():
                    for core in (0, 1):
                        b = block_of(stream, d, core)
                        relay_copy(b, j, way).wait_recv()

                        @pl.when(ring_next[way] != source)
                        def _():
                            relay_copy(b, j, way).start()

    steps = chunks * chips

    def body(step, carry):
        @pl.when(step < steps)
        def _():
            line_part(step)

        for way in (0, 1):
            late = step - LAG * hops[way]

            @pl.when((late >= 0) & (late < steps))
            def _():
                ring_part(late, way)

        return carry

    lax.fori_loop(0, chunks, body, 0)
    for copy in small:
        copy.wait()
    capacity, (depth, slots) = x_ref.shape[0], choose_ref.shape
    place_of = slot_target(counts_ref, (1, slots), 1, capacity)
    choose = (lax.broadcasted_iota(jnp.int32, (depth, slots), 0) == place_of).astype(jnp.float32)
    gap = pick(cond_band, cond_energy) - pick(val_band, val_energy)
    gap = lax.dot_general(
        gap, choose, (((1,), (1,)), ((), ())), precision=lax.Precision.HIGHEST, preferred_element_type=jnp.float32
    )
    for f in range(weights_ref.shape[0]):
        weights_ref[f] = -4.0 * gap / (gap * gap + freq_ref[f] * freq_ref[f])
    choose_ref[...] = choose.astype(jnp.bfloat16)
    lax.fori_loop(chunks, steps + LAG * (cols - 1), body, 0)

    def finish(step, carry):
        d, j = step // chunks, step % chunks
        for stream in (0, 1):
            here = has(stream, d) if stream == 0 else has(stream, d) & (d > 0)
            b = block_of(stream, d, k)
            theirs = block_of(stream, d, 1 - k)

            @pl.when(has(stream, d) & onward(stream))
            def _():
                line_copy(stream, d, j, b).wait_send()

            @pl.when(here)
            def _():
                mate_copy(b, j).wait_send()
                mate_copy(theirs, j).wait_recv()

                @pl.when(feeds(j))
                def _():
                    for way in (0, 1):
                        enter_copy(b, j, way).wait_send()

                @pl.when(relays(j))
                def _():
                    for core in (0, 1):
                        e = block_of(stream, d, core)
                        for way in (0, 1):
                            @pl.when(ring_next[way] != source)
                            def _():
                                relay_copy(e, j, way).wait_send()

        return carry

    lax.fori_loop(0, steps, finish, 0)

    @pl.when(source == c)
    def _():
        here = pltpu.make_async_copy(cols_ref.at[:, pl.ds((r % ratio) * 2 * halves, 2 * halves)], seg_ref, own_sem.at[0])
        here.start()
        here.wait()


def gather(x, counts, frequency, val_band, cond_band, val_energy, cond_energy, rows, cols):
    capacity, width = x.shape
    slots = rows * capacity
    live = slots * 5 // 8
    depth = pl.cdiv(live, 256) * 256
    ratio = rows // cols
    seg_width = width // ratio
    halves = 2 if seg_width % 512 == 0 else 1
    chunks, chips = ratio * halves, rows // 2
    dma = pltpu.SemaphoreType.DMA
    return pl.pallas_call(
        functools.partial(gather_kernel, rows, cols, halves),
        out_shape=(
            pltpu.VMEM((rows, 2 * chunks, capacity, seg_width // halves // 2), x.dtype),
            pltpu.VMEM((rows, 2 * halves, capacity, seg_width // halves // 2), x.dtype),
            pltpu.VMEM((depth, slots), jnp.bfloat16),
            pltpu.VMEM((frequency.shape[0], 8, depth), jnp.float32),
        ),
        in_specs=[pl.BlockSpec(memory_space=pl.ANY)] * 7,
        out_specs=[pl.BlockSpec(memory_space=pltpu.VMEM)] * 4,
        scratch_shapes=[
            pltpu.SMEM(counts.shape, counts.dtype),
            pltpu.SMEM(frequency.shape, frequency.dtype),
            pltpu.VMEM(val_band.shape, val_band.dtype),
            pltpu.VMEM(cond_band.shape, cond_band.dtype),
            pltpu.VMEM(val_energy.shape, val_energy.dtype),
            pltpu.VMEM(cond_energy.shape, cond_energy.dtype),
            dma((6,)),
            dma((2 * chunks,)),
            dma((2, chips, chunks)),
            dma((2, chips, chunks)),
            dma((rows, chunks)),
            dma((rows, chunks)),
            dma((rows, chunks, 2)),
            dma((rows, halves, 2)),
            dma((rows, halves, 2)),
        ],
        compiler_params=pltpu.CompilerParams(
            collective_id=0, has_side_effects=True, vmem_limit_bytes=40 * 1024 * 1024
        ),
    )(x, counts, frequency, val_band, cond_band, val_energy, cond_energy)


def exact_dot(a, b):
    return lax.dot_general(
        a, b, (((1,), (0,)), ((), ())), precision=lax.Precision.HIGHEST, preferred_element_type=jnp.float32
    )


def pick(band_ref, table_ref):
    levels, slots = table_ref.shape[0], band_ref.shape[0]
    hit = lax.broadcasted_iota(jnp.int32, (levels, slots), 0) == band_ref[...][None, :]
    return exact_dot(jnp.broadcast_to(table_ref[...][None, :], (8, levels)), hit.astype(jnp.float32))


def slot_target(counts_ref, shape, axis, capacity):
    slot = lax.broadcasted_iota(jnp.int32, shape, axis)
    target = jnp.full(shape, -1, jnp.int32)
    before = 0
    for block in range(counts_ref.shape[0]):
        inside = slot - block * capacity
        live = (inside >= 0) & (inside < counts_ref[block])
        target = jnp.where(live, inside + before, target)
        before = before + counts_ref[block]
    return target


def product_kernel(weights, choose_ref, seg_ref, cols_ref, out_ref, packed, turned, scaled):
    which, n = pl.program_id(0), pl.program_id(1)
    tile = out_ref.shape[2]
    rows, pieces, capacity, lane = cols_ref.shape
    slots = rows * capacity

    @pl.when((n == 0) & (which == 0))
    def _():
        choose = choose_ref[...]
        for p in range(pieces):
            piece = cols_ref[:, p].reshape(slots, lane)
            packed[:, p * lane : (p + 1) * lane] = jnp.dot(
                choose, piece, preferred_element_type=jnp.float32
            ).astype(jnp.bfloat16)
        for p in range(seg_ref.shape[1]):
            piece = seg_ref[:, p].reshape(slots, lane)
            turned[p * lane : (p + 1) * lane, :] = lax.dot_general(
                piece, choose, (((0,), (1,)), ((), ())), preferred_element_type=jnp.float32
            ).astype(jnp.bfloat16)

    @pl.when(n == 0)
    def _():
        scaled[...] = (turned[...].astype(jnp.float32) * weights[which][:1]).astype(jnp.bfloat16)

    start = pl.multiple_of(n * tile, tile)
    out_ref[0] = jnp.dot(scaled[...], packed[:, pl.ds(start, tile)], preferred_element_type=jnp.float32)


def product(weights, choose, seg, columns):
    freqs = weights.shape[0]
    rows, pieces, capacity, lane = columns.shape
    width, seg_width = pieces * lane, seg.shape[1] * lane
    depth = choose.shape[0]
    tile = math.gcd(width, TILE)
    vmem = pl.BlockSpec(memory_space=pltpu.VMEM)
    return pl.pallas_call(
        product_kernel,
        out_shape=jax.ShapeDtypeStruct((freqs, seg_width, width), jnp.float32),
        grid=(freqs, width // tile),
        in_specs=[vmem] * 4,
        out_specs=pl.BlockSpec((1, seg_width, tile), lambda f, n: (f, 0, n)),
        scratch_shapes=[
            pltpu.VMEM((depth, width), jnp.bfloat16),
            pltpu.VMEM((seg_width, depth), jnp.bfloat16),
            pltpu.VMEM((seg_width, depth), jnp.bfloat16),
        ],
        compiler_params=pltpu.CompilerParams(vmem_limit_bytes=40 * 1024 * 1024),
    )(weights, choose, seg, columns)


def per_device(pair_elems, counts, val_band, cond_band, val_energy, cond_energy, frequency):
    rows, cols = lax.axis_size("row"), lax.axis_size("col")
    columns, seg, choose, weights = gather(
        pair_elems, counts, frequency, val_band, cond_band, val_energy, cond_energy, rows, cols
    )
    return product(weights, choose, seg, columns)


def solution(mesh):
    in_specs = (P("row", "col"), P(), P(), P(), P(), P(), P())
    out_specs = P(None, "row", "col")
    return jax.shard_map(
        per_device, mesh=mesh, in_specs=in_specs, out_specs=out_specs, check_vma=False
    )
```
